32 devices in a mesh: dp: 8 (over z, y), tensor: 4 (over x, core).
Axes of the slice: x: 2, y: 2, z: 4, core: 2. Of those that a mesh axis runs over, the one named last changes fastest.
Arguments:
- tokens: bfloat16 [2048, 1024], P('dp'), may hold values from -6 to 6
- norm_first: float32 [1024], replicated, may hold values from 0.25 to 1.75
- w_in: bfloat16 [1024, 3, 1024], P(None, None, 'tensor'), may hold values from -0.1875 to 0.1875
- conv_taps: float32 [3, 1024], P(None, 'tensor'), may hold values from -1 to 1
- w_out: bfloat16 [1024, 1024], P('tensor'), may hold values from -0.1875 to 0.1875
- norm_second: float32 [1024], replicated, may hold values from 0.25 to 1.75
- w_gate_up: bfloat16 [1024, 2, 4608], P(None, None, 'tensor'), may hold values from -0.1875 to 0.1875
- w_down: bfloat16 [4608, 1024], P('tensor'), may hold values from -0.09375 to 0.09375
- cotangent: bfloat16 [2048, 1024], P('dp'), may hold values from -6 to 6
Outputs:
- block_out: bfloat16 [2048, 1024], P('dp')
- grad_tokens: float32 [2048, 1024], P('dp')
- grad_norm_first: float32 [1024], replicated
- grad_w_in: float32 [1024, 3, 1024], P('dp', None, 'tensor')
- grad_taps: float32 [3, 1024], P(None, 'tensor')
- grad_w_out: float32 [1024, 1024], P('tensor', 'dp')
- grad_norm_second: float32 [1024], replicated
- grad_w_gate_up: float32 [1024, 2, 4608], P('dp', None, 'tensor')
- grad_w_down: float32 [4608, 1024], P('tensor', 'dp')
The draws below stay inside these ranges and needn't reach their ends.
All inputs are finite; a program needn't handle non-finite values.
Results may differ from the reference program's by a relative error of at most 0.011.
Values sent between devices are 32-bit elements; how exact they have to be, the bound alone decides.
No kernel may reach another device: no remote copies, remote signals or barrier semaphores. Data moves between devices by JAX's collectives and lax.ppermute only.
A program may use at most 128 MiB of HBM per device.

```python
import jax
import jax.numpy as jnp
from jax import lax

D = 1024
FF = 4608
TAPS = 3
TOK_DEV = 256
SEQS = 8
TOKENS = 2048


def strengthened(array, stream_key, source, target, shards_of, factor):
    owner, partner = [(jnp.arange(array.shape[position]) // (array.shape[position] // shards_of)).reshape([-1 if axis == position else 1 for axis in range(array.ndim)]) for position in (source, target)]
    chosen = jax.random.permutation(stream_key, shards_of)[partner]
    strong = (owner == chosen) | (owner == (partner + shards_of // 2) % shards_of)
    return jnp.where(strong, factor * array, array)


def steps_of(key, dims, pieces, smallest, high):
    def one(axis_at, blocks):
        draws = jax.random.uniform(jax.random.fold_in(jax.random.fold_in(key, 6), axis_at), (blocks,), jnp.float32, smallest / len(pieces), high / len(pieces))
        return jnp.repeat(jnp.exp(draws), dims[axis_at] // blocks).reshape((-1,) + (1,) * (len(dims) - axis_at - 1))

    level = one(*pieces[0])
    for cut in pieces[1:]:
        level = level * one(*cut)
    return level


def centred(rng, dims, scale, most, pieces=(), kind=jnp.bfloat16):
    level = steps_of(rng, dims, pieces, -0.22, 0.18) if pieces else 1.0
    array = jax.random.normal(rng, dims, jnp.float32) * scale * level
    return jnp.minimum(jnp.maximum(array, -most), most).astype(kind)


def heavy_noise(stream_key, shape, deviation, reach, split, heavy, kind=jnp.bfloat16):
    array = deviation * jax.random.normal(stream_key, shape, jnp.float32)
    if split:
        array = array * steps_of(stream_key, shape, split, -0.22, 0.18)
    return jnp.clip(strengthened(array, jax.random.fold_in(stream_key, 3), *heavy), -reach, reach).astype(kind)


def setup_inputs(seed: int = 0) -> dict:
    key_list = jax.random.split(jax.random.key(seed), 10)
    tokens = centred(key_list[0], (TOKENS, D), 1.0, 6.0, ((0, 8),))
    norm_first = jnp.clip(1.0 + 0.15 * jax.random.normal(key_list[1], (D,), jnp.float32), 0.25, 1.75)
    w_in = centred(key_list[2], (D, 3, D), D ** -0.5, 0.1875, ((2, 4),))
    conv_taps = jnp.clip(jax.random.uniform(key_list[3], (TAPS, D), jnp.float32, -1.0, 1.0) * steps_of(key_list[3], (TAPS, D), ((1, 4),), -0.4, 0.0), -1.0, 1.0)
    w_out = centred(key_list[4], (D, D), D ** -0.5, 0.1875, ((0, 4),))
    norm_second = jnp.clip(1.0 + 0.15 * jax.random.normal(key_list[5], (D,), jnp.float32), 0.25, 1.75)
    w_gate_up = centred(key_list[6], (D, 2, FF), D ** -0.5, 0.1875, ((2, 4),))
    w_down = centred(key_list[7], (FF, D), FF ** -0.5, 0.09375, ((0, 4),))
    cotangent = heavy_noise(key_list[8], (TOKENS, D), 1.0, 6.0, ((0, 8),), (0, 1, 8, 2.0))
    return dict(tokens=tokens, norm_first=norm_first, w_in=w_in, conv_taps=conv_taps, w_out=w_out, norm_second=norm_second, w_gate_up=w_gate_up, w_down=w_down, cotangent=cotangent)


eps = 1e-05

def shift_down(values, count):
    pad = jnp.zeros((count, values.shape[1]), values.dtype)
    return jnp.concatenate([pad, values[:values.shape[0] - count]], axis=0)

def shift_up(values, count):
    pad = jnp.zeros((count, values.shape[1]), values.dtype)
    return jnp.concatenate([values[count:], pad], axis=0)

def cross(left, right):
    return lax.dot_general(left, right, (((0,), (0,)), ((), ())), preferred_element_type=jnp.float32)

def by_transpose(left, right):
    return lax.dot_general(left, right, (((1,), (1,)), ((), ())), preferred_element_type=jnp.float32)

def reference(tokens, norm_first, w_in, conv_taps, w_out, norm_second, w_gate_up, w_down, cotangent):
    width = tokens.shape[1]
    w_in_flat = w_in.reshape(width, -1)
    w_gu_flat = w_gate_up.reshape(width, -1)
    hid = w_down.shape[0]
    seq_tokens = tokens.reshape(SEQS, TOK_DEV, width)
    seq_cot = cotangent.reshape(SEQS, TOK_DEV, width)

    def one(carry, item):
        g_in, g_out, g_gu, g_down, g_taps, g_n1, g_n2 = carry
        tok, cot = item
        xf = tok.astype(jnp.float32)
        s1 = lax.rsqrt(lax.optimization_barrier(jnp.mean(xf * xf, axis=-1, keepdims=True)) + eps)
        normed1 = (xf * s1 * norm_first).astype(jnp.bfloat16)
        proj = jnp.dot(normed1, w_in_flat, preferred_element_type=jnp.float32).reshape(TOK_DEV, 3, width)
        gate_b, gate_c, value = (proj[:, 0], proj[:, 1], proj[:, 2])
        mixed_in = gate_b * value
        conv = conv_taps[0] * shift_down(mixed_in, 2) + conv_taps[1] * shift_down(mixed_in, 1) + conv_taps[2] * mixed_in
        gated = (gate_c * conv).astype(jnp.bfloat16)
        resid = xf + jnp.dot(gated, w_out, preferred_element_type=jnp.float32)
        s2 = lax.rsqrt(lax.optimization_barrier(jnp.mean(resid * resid, axis=-1, keepdims=True)) + eps)
        normed2 = (resid * s2 * norm_second).astype(jnp.bfloat16)
        gu = jnp.dot(normed2, w_gu_flat, preferred_element_type=jnp.float32).reshape(TOK_DEV, 2, hid)
        act, up = (gu[:, 0], gu[:, 1])
        sig = jax.nn.sigmoid(act)
        hidden = (act * sig * up).astype(jnp.bfloat16)
        out = (resid + jnp.dot(hidden, w_down, preferred_element_type=jnp.float32)).astype(jnp.bfloat16)
        cotf = cot.astype(jnp.float32)
        grad_down = cross(hidden, cot)
        d_hidden = by_transpose(cot, w_down)
        d_act = d_hidden * up * sig * (1.0 + act * (1.0 - sig))
        d_up = d_hidden * act * sig
        d_gu = jnp.stack([d_act, d_up], axis=1).astype(jnp.bfloat16).reshape(TOK_DEV, 2 * hid)
        grad_gu = cross(normed2, d_gu)
        d_normed2 = by_transpose(d_gu, w_gu_flat)
        gn2 = lax.optimization_barrier(jnp.sum(d_normed2 * resid * s2, axis=0))
        w2 = d_normed2 * norm_second
        d_resid = cotf + s2 * w2 - resid * s2 ** 3 * lax.optimization_barrier(jnp.mean(w2 * resid, axis=-1, keepdims=True))
        d_resid_b = d_resid.astype(jnp.bfloat16)
        grad_out = cross(gated, d_resid_b)
        d_gated = by_transpose(d_resid_b, w_out)
        d_c = d_gated * conv
        d_conv = d_gated * gate_c
        gtaps = jnp.stack([lax.optimization_barrier(jnp.sum(d_conv * shift_down(mixed_in, 2), axis=0)), lax.optimization_barrier(jnp.sum(d_conv * shift_down(mixed_in, 1), axis=0)), lax.optimization_barrier(jnp.sum(d_conv * mixed_in, axis=0))], axis=0)
        d_mixed = conv_taps[2] * d_conv + conv_taps[1] * shift_up(d_conv, 1) + conv_taps[0] * shift_up(d_conv, 2)
        d_proj = jnp.stack([d_mixed * value, d_c, d_mixed * gate_b], axis=1).astype(jnp.bfloat16).reshape(TOK_DEV, 3 * width)
        grad_in = cross(normed1, d_proj)
        d_normed1 = by_transpose(d_proj, w_in_flat)
        gn1 = lax.optimization_barrier(jnp.sum(d_normed1 * xf * s1, axis=0))
        w1 = d_normed1 * norm_first
        d_tok = d_resid + s1 * w1 - xf * s1 ** 3 * lax.optimization_barrier(jnp.mean(w1 * xf, axis=-1, keepdims=True))
        carry = (g_in + grad_in, g_out + grad_out, g_gu + grad_gu, g_down + grad_down, g_taps + gtaps, g_n1 + gn1, g_n2 + gn2)
        return (carry, (out, d_tok))
    init = (jnp.zeros((width, 3 * width), jnp.float32), jnp.zeros((width, width), jnp.float32), jnp.zeros((width, 2 * hid), jnp.float32), jnp.zeros((hid, width), jnp.float32), jnp.zeros((3, width), jnp.float32), jnp.zeros((width,), jnp.float32), jnp.zeros((width,), jnp.float32))
    carry, (outs, d_toks) = lax.scan(one, init, (seq_tokens, seq_cot))
    g_in, g_out, g_gu, g_down, g_taps, g_n1, g_n2 = carry
    return (outs.reshape(-1, width), d_toks.reshape(-1, width), g_n1, g_in.reshape(width, 3, width), g_taps, g_out, g_n2, g_gu.reshape(width, 2, hid), g_down)
```

```python
import jax
import jax.numpy as jnp
from jax import lax
from jax.sharding import PartitionSpec as P

eps = 1e-05


def shift_down(values, count):
    pad = jnp.zeros((count, values.shape[1]), values.dtype)
    return jnp.concatenate([pad, values[: values.shape[0] - count]], axis=0)


def shift_up(values, count):
    pad = jnp.zeros((count, values.shape[1]), values.dtype)
    return jnp.concatenate([values[count:], pad], axis=0)


def cross(left, right):
    return lax.dot_general(
        left, right, (((0,), (0,)), ((), ())), preferred_element_type=jnp.float32
    )


def by_transpose(left, right):
    return lax.dot_general(
        left, right, (((1,), (1,)), ((), ())), preferred_element_type=jnp.float32
    )


def body_scatter(tokens, norm_first, w_in, conv_taps, w_out, norm_second, w_gate_up, w_down, cotangent):
    rows, width = tokens.shape
    chans = w_in.shape[2]
    hid = w_down.shape[0]
    w_in_flat = w_in.reshape(width, 3 * chans)
    w_gu_flat = w_gate_up.reshape(width, 2 * hid)
    xf = tokens.astype(jnp.float32)
    s1 = lax.rsqrt(jnp.mean(xf * xf, axis=-1, keepdims=True) + eps)
    normed1 = (xf * s1 * norm_first).astype(jnp.bfloat16)
    proj = jnp.dot(normed1, w_in_flat, preferred_element_type=jnp.float32).reshape(rows, 3, chans)
    gate_b, gate_c, value = (proj[:, 0], proj[:, 1], proj[:, 2])
    mixed_in = gate_b * value
    conv = (
        conv_taps[0] * shift_down(mixed_in, 2)
        + conv_taps[1] * shift_down(mixed_in, 1)
        + conv_taps[2] * mixed_in
    )
    gated = (gate_c * conv).astype(jnp.bfloat16)
    mix = lax.psum(jnp.dot(gated, w_out, preferred_element_type=jnp.float32), "tensor")
    resid = xf + mix
    s2 = lax.rsqrt(jnp.mean(resid * resid, axis=-1, keepdims=True) + eps)
    normed2 = (resid * s2 * norm_second).astype(jnp.bfloat16)
    gate_up = jnp.dot(normed2, w_gu_flat, preferred_element_type=jnp.float32).reshape(rows, 2, hid)
    act, up = (gate_up[:, 0], gate_up[:, 1])
    sig = jax.nn.sigmoid(act)
    hidden = (act * sig * up).astype(jnp.bfloat16)
    ffn = lax.psum(jnp.dot(hidden, w_down, preferred_element_type=jnp.float32), "tensor")
    block_out = (resid + ffn).astype(jnp.bfloat16)
    cotf = cotangent.astype(jnp.float32)
    grad_down = cross(hidden, cotangent)
    d_hidden = by_transpose(cotangent, w_down)
    d_act = d_hidden * up * sig * (1.0 + act * (1.0 - sig))
    d_up = d_hidden * act * sig
    d_gu = jnp.stack([d_act, d_up], axis=1).astype(jnp.bfloat16).reshape(rows, 2 * hid)
    grad_gu = cross(normed2, d_gu).reshape(width, 2, hid)
    d_normed2 = lax.psum(by_transpose(d_gu, w_gu_flat), "tensor")
    gn2 = jnp.sum(d_normed2 * resid * s2, axis=0)
    weighted2 = d_normed2 * norm_second
    d_resid = (
        cotf + s2 * weighted2 - resid * s2**3 * jnp.mean(weighted2 * resid, axis=-1, keepdims=True)
    )
    d_resid_b = d_resid.astype(jnp.bfloat16)
    grad_out = cross(gated, d_resid_b)
    d_gated = by_transpose(d_resid_b, w_out)
    d_c = d_gated * conv
    d_conv = d_gated * gate_c
    gtaps = jnp.stack(
        [
            jnp.sum(d_conv * shift_down(mixed_in, 2), axis=0),
            jnp.sum(d_conv * shift_down(mixed_in, 1), axis=0),
            jnp.sum(d_conv * mixed_in, axis=0),
        ],
        axis=0,
    )
    d_mixed = (
        conv_taps[2] * d_conv
        + conv_taps[1] * shift_up(d_conv, 1)
        + conv_taps[0] * shift_up(d_conv, 2)
    )
    d_proj = (
        jnp.stack([d_mixed * value, d_c, d_mixed * gate_b], axis=1)
        .astype(jnp.bfloat16)
        .reshape(rows, 3 * chans)
    )
    grad_in = cross(normed1, d_proj).reshape(width, 3, chans)
    d_normed1 = lax.psum(by_transpose(d_proj, w_in_flat), "tensor")
    gn1 = jnp.sum(d_normed1 * xf * s1, axis=0)
    weighted1 = d_normed1 * norm_first
    grad_tokens = (
        d_resid + s1 * weighted1 - xf * s1**3 * jnp.mean(weighted1 * xf, axis=-1, keepdims=True)
    )
    shared_in, shared_out, shared_gu, shared_down = (
        lax.psum_scatter(grad_in, "dp", scatter_dimension=0, tiled=True),
        lax.psum_scatter(grad_out, "dp", scatter_dimension=1, tiled=True),
        lax.psum_scatter(grad_gu, "dp", scatter_dimension=0, tiled=True),
        lax.psum_scatter(grad_down, "dp", scatter_dimension=1, tiled=True),
    )
    sum_taps, sum_n1, sum_n2 = lax.psum((gtaps, gn1, gn2), "dp")
    return (
        block_out,
        grad_tokens,
        sum_n1,
        shared_in,
        sum_taps,
        shared_out,
        sum_n2,
        shared_gu,
        shared_down,
    )


def body_gather(
    dp,
    tensor,
    tokens,
    norm_first,
    w_in,
    conv_taps,
    w_out,
    norm_second,
    w_gate_up,
    w_down,
    cotangent,
):
    rows, width = tokens.shape
    chans = w_in.shape[2]
    hid = w_down.shape[0]
    half = rows // 2
    line = dp // 2
    block = width // dp
    f32, bf16 = jnp.float32, jnp.bfloat16
    w_in_flat = w_in.reshape(width, 3 * chans)
    w_gu_flat = w_gate_up.reshape(width, 2 * hid)
    core = lax.axis_index("tensor") % 2
    place = lax.axis_index("dp")
    along, side = place // 2, place % 2

    def to_core(values):
        return lax.ppermute(values, "tensor", [(i, i ^ 1) for i in range(tensor)])

    def to_side(values):
        return lax.ppermute(values, "dp", [(i, i ^ 1) for i in range(dp)])

    def to_line(values, count):
        return lax.ppermute(
            values, "dp", [(i, (i + 2 * count) % dp) for i in range(dp)]
        )

    def over_chips(values):
        stride = 2
        while stride < tensor:
            values = values + lax.ppermute(
                values, "tensor", [(i, i ^ stride) for i in range(tensor)]
            )
            stride *= 2
        return values

    def mine(values):
        return lax.dynamic_slice_in_dim(values, core * half, half, 0)

    def other(values):
        return lax.dynamic_slice_in_dim(values, (1 - core) * half, half, 0)

    is_second = core.astype(f32)
    is_first = 1.0 - is_second

    def ordered(own, partner):
        return jnp.concatenate(
            [own * is_first + partner * is_second, own * is_second + partner * is_first], axis=0
        )

    def gathered(values):
        near = jnp.concatenate([to_line(values, k) for k in range(1, line)], axis=0)
        return near, to_core(near)

    def conv_forward(tok):
        s1 = lax.rsqrt(jnp.mean(tok * tok, axis=-1, keepdims=True) + eps)
        normed1 = (tok * s1 * norm_first).astype(bf16)
        proj = jnp.dot(normed1, w_in_flat, preferred_element_type=f32)
        gate_b, gate_c, value = (
            proj[:, :chans],
            proj[:, chans : 2 * chans],
            proj[:, 2 * chans :],
        )
        mixed_in = gate_b * value
        conv = (
            conv_taps[0] * shift_down(mixed_in, 2)
            + conv_taps[1] * shift_down(mixed_in, 1)
            + conv_taps[2] * mixed_in
        )
        gated = (gate_c * conv).astype(bf16)
        return s1, normed1, gate_b, gate_c, value, mixed_in, conv, gated

    def conv_backward(d_resid_b, saved):
        _, _, gate_b, gate_c, value, mixed_in, conv, _ = saved
        d_gated = by_transpose(d_resid_b, w_out)
        d_c = d_gated * conv
        d_conv = d_gated * gate_c
        gtaps = jnp.stack(
            [
                jnp.sum(d_conv * shift_down(mixed_in, 2), axis=0),
                jnp.sum(d_conv * shift_down(mixed_in, 1), axis=0),
                jnp.sum(d_conv * mixed_in, axis=0),
            ],
            axis=0,
        )
        d_mixed = (
            conv_taps[2] * d_conv
            + conv_taps[1] * shift_up(d_conv, 1)
            + conv_taps[0] * shift_up(d_conv, 2)
        )
        d_proj = jnp.concatenate([d_mixed * value, d_c, d_mixed * gate_b], axis=1).astype(bf16)
        return d_proj, gtaps

    def ffn(normed2, cot):
        gate_up = jnp.dot(normed2, w_gu_flat, preferred_element_type=f32)
        act, up = gate_up[:, :hid], gate_up[:, hid:]
        sig = jax.nn.sigmoid(act)
        hidden = (act * sig * up).astype(bf16)
        d_hidden = by_transpose(cot, w_down)
        d_act = d_hidden * up * sig * (1.0 + act * (1.0 - sig))
        d_up = d_hidden * act * sig
        return hidden, jnp.concatenate([d_act, d_up], axis=1).astype(bf16)

    xf = tokens.astype(f32)
    cotf = cotangent.astype(f32)
    cot_mine = mine(cotf)
    cot_far = ordered(*gathered(cot_mine)).astype(bf16)
    beside = to_side(xf)

    saved = conv_forward(xf)
    s1, normed1, gated = saved[0], saved[1], saved[7]
    mix = jnp.dot(gated, w_out, preferred_element_type=f32)
    mix = over_chips(mine(mix) + to_core(other(mix)))
    saved_beside = conv_forward(beside)

    resid = mine(xf) + mix
    s2 = lax.rsqrt(jnp.mean(resid * resid, axis=-1, keepdims=True) + eps)
    scaled = resid * s2
    normed2_near = (jnp.concatenate([scaled, to_core(scaled)], axis=0) * norm_second).astype(bf16)
    normed2_far = (ordered(*gathered(scaled)) * norm_second).astype(bf16)

    cot_near = jnp.concatenate([mine(cotangent), other(cotangent)], axis=0)
    hidden_near, d_gu_near = ffn(normed2_near, cot_near)
    d_normed2 = by_transpose(d_gu_near, w_gu_flat)
    d_normed2 = over_chips(d_normed2[:half] + to_core(d_normed2[half:]))
    gn2 = jnp.sum(d_normed2 * resid * s2, axis=0)
    weighted2 = d_normed2 * norm_second
    d_resid = (
        cot_mine
        + s2 * weighted2
        - resid * s2**3 * jnp.mean(weighted2 * resid, axis=-1, keepdims=True)
    )
    d_resid_seq = ordered(d_resid, to_core(d_resid)).astype(bf16)
    d_resid_beside = to_side(d_resid)
    d_resid_next = ordered(d_resid_beside, to_core(d_resid_beside)).astype(bf16)

    d_proj, gtaps = conv_backward(d_resid_seq, saved)
    d_normed1 = by_transpose(d_proj, w_in_flat)
    d_normed1 = over_chips(mine(d_normed1) + to_core(other(d_normed1)))
    xf_mine, s1_mine = mine(xf), mine(s1)
    gn1 = jnp.sum(d_normed1 * xf_mine * s1_mine, axis=0)
    weighted1 = d_normed1 * norm_first
    grad_mine = (
        d_resid
        + s1_mine * weighted1
        - xf_mine * s1_mine**3 * jnp.mean(weighted1 * xf_mine, axis=-1, keepdims=True)
    )
    grad_tokens = ordered(grad_mine, to_core(grad_mine))

    out = jnp.dot(hidden_near, w_down, preferred_element_type=f32)
    out = over_chips(out[:half] + to_core(out[half:]))
    out_mine = resid + out
    block_out = ordered(out_mine, to_core(out_mine)).astype(bf16)

    hidden_far, d_gu_far = ffn(normed2_far, cot_far)
    own_at, side_at = place * block, (along * 2 + 1 - side) * block

    def columns(values, start):
        return lax.dynamic_slice_in_dim(values, start, block, 1)

    def gu_part(start):
        return cross(columns(normed2_near, start), d_gu_near) + cross(
            columns(normed2_far, start), d_gu_far
        )

    def down_part(start):
        return cross(hidden_near, columns(cot_near, start)) + cross(
            hidden_far, columns(cot_far, start)
        )

    grad_down = down_part(own_at) + to_side(down_part(side_at))
    grad_gu = gu_part(own_at) + to_side(gu_part(side_at))

    d_proj_beside, _ = conv_backward(d_resid_next, saved_beside)

    def spread(first, second):
        both = jnp.concatenate([first, second], axis=0).reshape(2 * rows, line, 2, block)
        both = lax.dynamic_index_in_dim(both, side, 2, keepdims=False)
        both = jnp.concatenate([both, both], axis=1)
        both = lax.dynamic_slice_in_dim(both, along, line, 1)
        return both.reshape(2 * rows, line * block)

    part = jnp.concatenate(
        [
            cross(spread(normed1, saved_beside[1]), jnp.concatenate([d_proj, d_proj_beside], axis=0)),
            cross(
                spread(d_resid_seq, d_resid_next),
                jnp.concatenate([gated, saved_beside[7]], axis=0),
            ),
        ],
        axis=1,
    )
    total = part[:block]
    for k in range(1, line):
        total = total + to_line(part[k * block : (k + 1) * block], k)
    grad_in = total[:, : 3 * chans].reshape(block, 3, chans)
    grad_out = total[:, 3 * chans :].T

    gains = jnp.concatenate([gn1, gn2]).reshape(2, width)
    gains = gains + to_core(gains)
    small = jnp.concatenate([gains.reshape(-1), gtaps.reshape(-1)])
    stride = 1
    while stride < dp:
        small = small + lax.ppermute(small, "dp", [(i, i ^ stride) for i in range(dp)])
        stride *= 2
    return (
        block_out,
        grad_tokens,
        small[:width],
        grad_in,
        small[2 * width :].reshape(gtaps.shape),
        grad_out,
        small[width : 2 * width],
        grad_gu.reshape(block, 2, hid),
        grad_down,
    )


def solution(mesh):
    dp, tensor = mesh.shape["dp"], mesh.shape["tensor"]

    def body(*args):
        rows, width = args[0].shape
        line = dp // 2
        gathers = (
            dp % 2 == 0
            and line & (line - 1) == 0
            and tensor > 1
            and tensor & (tensor - 1) == 0
            and rows % 2 == 0
            and width % dp == 0
            and dp * rows <= 2 * width
        )
        if gathers:
            return body_gather(dp, tensor, *args)
        return body_scatter(*args)

    return jax.shard_map(
        body,
        mesh=mesh,
        in_specs=(
            P("dp", None),
            P(),
            P(None, None, "tensor"),
            P(None, "tensor"),
            P("tensor", None),
            P(),
            P(None, None, "tensor"),
            P("tensor", None),
            P("dp", None),
        ),
        out_specs=(
            P("dp", None),
            P("dp", None),
            P(),
            P("dp", None, "tensor"),
            P(None, "tensor"),
            P("tensor", "dp"),
            P(),
            P("dp", None, "tensor"),
            P("tensor", "dp"),
        ),
        check_vma=False,
    )
```

```python
import functools

import jax
import jax.numpy as jnp
from jax import lax
from jax.experimental import pallas as pl
from jax.experimental.pallas import tpu as pltpu
from jax.sharding import PartitionSpec as P


eps = 1e-05


def shift_down(values, count):
    pad = jnp.zeros((count, values.shape[1]), values.dtype)
    return jnp.concatenate([pad, values[: values.shape[0] - count]], axis=0)


def shift_up(values, count):
    pad = jnp.zeros((count, values.shape[1]), values.dtype)
    return jnp.concatenate([values[count:], pad], axis=0)


def cross(left, right):
    return lax.dot_general(
        left, right, (((0,), (0,)), ((), ())), preferred_element_type=jnp.float32
    )


def by_transpose(left, right):
    return lax.dot_general(
        left, right, (((1,), (1,)), ((), ())), preferred_element_type=jnp.float32
    )


def body_scatter(tokens, norm_first, w_in, conv_taps, w_out, norm_second, w_gate_up, w_down, cotangent):
    rows, width = tokens.shape
    chans = w_in.shape[2]
    hid = w_down.shape[0]
    w_in_flat = w_in.reshape(width, 3 * chans)
    w_gu_flat = w_gate_up.reshape(width, 2 * hid)
    xf = tokens.astype(jnp.float32)
    s1 = lax.rsqrt(jnp.mean(xf * xf, axis=-1, keepdims=True) + eps)
    normed1 = (xf * s1 * norm_first).astype(jnp.bfloat16)
    proj = jnp.dot(normed1, w_in_flat, preferred_element_type=jnp.float32).reshape(rows, 3, chans)
    gate_b, gate_c, value = (proj[:, 0], proj[:, 1], proj[:, 2])
    mixed_in = gate_b * value
    conv = (
        conv_taps[0] * shift_down(mixed_in, 2)
        + conv_taps[1] * shift_down(mixed_in, 1)
        + conv_taps[2] * mixed_in
    )
    gated = (gate_c * conv).astype(jnp.bfloat16)
    mix = lax.psum(jnp.dot(gated, w_out, preferred_element_type=jnp.float32), "tensor")
    resid = xf + mix
    s2 = lax.rsqrt(jnp.mean(resid * resid, axis=-1, keepdims=True) + eps)
    normed2 = (resid * s2 * norm_second).astype(jnp.bfloat16)
    gate_up = jnp.dot(normed2, w_gu_flat, preferred_element_type=jnp.float32).reshape(rows, 2, hid)
    act, up = (gate_up[:, 0], gate_up[:, 1])
    sig = jax.nn.sigmoid(act)
    hidden = (act * sig * up).astype(jnp.bfloat16)
    ffn = lax.psum(jnp.dot(hidden, w_down, preferred_element_type=jnp.float32), "tensor")
    block_out = (resid + ffn).astype(jnp.bfloat16)
    cotf = cotangent.astype(jnp.float32)
    grad_down = cross(hidden, cotangent)
    d_hidden = by_transpose(cotangent, w_down)
    d_act = d_hidden * up * sig * (1.0 + act * (1.0 - sig))
    d_up = d_hidden * act * sig
    d_gu = jnp.stack([d_act, d_up], axis=1).astype(jnp.bfloat16).reshape(rows, 2 * hid)
    grad_gu = cross(normed2, d_gu).reshape(width, 2, hid)
    d_normed2 = lax.psum(by_transpose(d_gu, w_gu_flat), "tensor")
    gn2 = jnp.sum(d_normed2 * resid * s2, axis=0)
    weighted2 = d_normed2 * norm_second
    d_resid = (
        cotf + s2 * weighted2 - resid * s2**3 * jnp.mean(weighted2 * resid, axis=-1, keepdims=True)
    )
    d_resid_b = d_resid.astype(jnp.bfloat16)
    grad_out = cross(gated, d_resid_b)
    d_gated = by_transpose(d_resid_b, w_out)
    d_c = d_gated * conv
    d_conv = d_gated * gate_c
    gtaps = jnp.stack(
        [
            jnp.sum(d_conv * shift_down(mixed_in, 2), axis=0),
            jnp.sum(d_conv * shift_down(mixed_in, 1), axis=0),
            jnp.sum(d_conv * mixed_in, axis=0),
        ],
        axis=0,
    )
    d_mixed = (
        conv_taps[2] * d_conv
        + conv_taps[1] * shift_up(d_conv, 1)
        + conv_taps[0] * shift_up(d_conv, 2)
    )
    d_proj = (
        jnp.stack([d_mixed * value, d_c, d_mixed * gate_b], axis=1)
        .astype(jnp.bfloat16)
        .reshape(rows, 3 * chans)
    )
    grad_in = cross(normed1, d_proj).reshape(width, 3, chans)
    d_normed1 = lax.psum(by_transpose(d_proj, w_in_flat), "tensor")
    gn1 = jnp.sum(d_normed1 * xf * s1, axis=0)
    weighted1 = d_normed1 * norm_first
    grad_tokens = (
        d_resid + s1 * weighted1 - xf * s1**3 * jnp.mean(weighted1 * xf, axis=-1, keepdims=True)
    )
    shared_in, shared_out, shared_gu, shared_down = (
        lax.psum_scatter(grad_in, "dp", scatter_dimension=0, tiled=True),
        lax.psum_scatter(grad_out, "dp", scatter_dimension=1, tiled=True),
        lax.psum_scatter(grad_gu, "dp", scatter_dimension=0, tiled=True),
        lax.psum_scatter(grad_down, "dp", scatter_dimension=1, tiled=True),
    )
    sum_taps, sum_n1, sum_n2 = lax.psum((gtaps, gn1, gn2), "dp")
    return (
        block_out,
        grad_tokens,
        sum_n1,
        shared_in,
        sum_taps,
        shared_out,
        sum_n2,
        shared_gu,
        shared_down,
    )


def gathers(dp, tensor, rows, width, hid):
    powers = all(size > 1 and size & (size - 1) == 0 for size in (dp, tensor))
    whole = rows % (8 * tensor) == 0 and hid % (128 * tensor) == 0
    return powers and whole and width % (128 * dp) == 0 and dp * rows <= 2 * width


def far_kernel(
    where,
    *refs,
    rows,
    share,
    block,
):
    pieces, refs = refs[:8], refs[8:]
    norm, x_near, c_near, h_near, dg_near, du_near, wg, wu, wd = refs[:9]
    gu_own, gu_there, down_own, down_there, x_all, c_all, xs, cs, dg, du, hidden = refs[9:]
    f32, bf16 = jnp.float32, jnp.bfloat16

    @pl.when(pl.program_id(0) == 0)
    def _():
        x_all[:rows] = x_near[...]
        c_all[:rows] = c_near[...]
        for i in range(4):
            at = pl.ds(rows + i * share, share)
            x_all[at] = (pieces[i][...] * norm[...]).astype(bf16)
            c_all[at] = pieces[4 + i][...].astype(bf16)
        for i in range(2):
            at = pl.ds(pl.multiple_of(where[i] * block, block), block)
            xs[:, i * block : (i + 1) * block] = x_all[:, at]
            cs[:, i * block : (i + 1) * block] = c_all[:, at]

    act = jnp.dot(x_all[rows:], wg[...], preferred_element_type=f32)
    up = jnp.dot(x_all[rows:], wu[...], preferred_element_type=f32)
    d_hidden = by_transpose(c_all[rows:], wd[...])
    sig = jax.nn.sigmoid(act)
    hidden[:rows] = h_near[...]
    dg[:rows] = dg_near[...]
    du[:rows] = du_near[...]
    hidden[rows:] = (act * sig * up).astype(bf16)
    dg[rows:] = (d_hidden * up * sig * (1.0 + act * (1.0 - sig))).astype(bf16)
    du[rows:] = (d_hidden * act * sig).astype(bf16)
    for i, grad in enumerate((dg, du)):
        both = cross(xs[...], grad[...])
        gu_own[i] = both[:block]
        gu_there[i] = both[block:]
    both = cross(hidden[...], cs[...])
    down_own[...] = both[:, :block]
    down_there[...] = both[:, block:]


def far_grads(where, pieces, norm, x_near, c_near, h_near, d_gu_near, w_gu, w_down):
    rows, width = x_near.shape
    hid = w_down.shape[0]
    share = pieces[0].shape[0]
    block = 128
    tokens = rows + 4 * share
    step = max(size for size in range(128, 513, 128) if hid % size == 0)
    steps = hid // step
    f32, bf16 = jnp.float32, jnp.bfloat16

    def whole(array):
        return pl.BlockSpec(
            array.shape, lambda j, _: (0,) * array.ndim, pipeline_mode=pl.Buffered(1)
        )

    return pl.pallas_call(
        functools.partial(far_kernel, rows=rows, share=share, block=block),
        out_shape=(
            *[jax.ShapeDtypeStruct((2, block, hid), f32)] * 2,
            *[jax.ShapeDtypeStruct((hid, block), f32)] * 2,
        ),
        grid_spec=pltpu.PrefetchScalarGridSpec(
            num_scalar_prefetch=1,
            grid=(steps,),
            in_specs=[
                *[whole(piece) for piece in pieces],
                whole(norm),
                whole(x_near),
                whole(c_near),
                pl.BlockSpec((rows, step), lambda j, _: (0, j)),
                pl.BlockSpec((rows, step), lambda j, _: (0, j)),
                pl.BlockSpec((rows, step), lambda j, _: (0, j + steps)),
                pl.BlockSpec((width, step), lambda j, _: (0, j)),
                pl.BlockSpec((width, step), lambda j, _: (0, j + steps)),
                pl.BlockSpec((step, width), lambda j, _: (j, 0)),
            ],
            out_specs=[
                *[pl.BlockSpec((2, block, step), lambda j, _: (0, 0, j))] * 2,
                *[pl.BlockSpec((step, block), lambda j, _: (j, 0))] * 2,
            ],
            scratch_shapes=[
                *[pltpu.VMEM((tokens, width), bf16)] * 2,
                *[pltpu.VMEM((tokens, 2 * block), bf16)] * 2,
                *[pltpu.VMEM((tokens, step), bf16)] * 3,
            ],
        ),
        compiler_params=pltpu.CompilerParams(vmem_limit_bytes=48 << 20),
        cost_estimate=pl.CostEstimate(
            flops=2 * hid * (3 * 4 * share * width + 3 * tokens * 2 * block),
            bytes_accessed=8 * share * width * 4 + 6 * hid * width + 24 * hid * block,
            transcendentals=4 * share * hid,
        ),
        name="far_grads",
    )(where, *pieces, norm, x_near, c_near, h_near, d_gu_near, d_gu_near, w_gu, w_gu, w_down)


def body_gather(
    dp,
    tensor,
    tokens,
    norm_first,
    w_in,
    conv_taps,
    w_out,
    norm_second,
    w_gate_up,
    w_down,
    cotangent,
):
    rows, width = tokens.shape
    chans = w_in.shape[2]
    hid = w_down.shape[0]
    half = rows // 2
    line = dp // 2
    block = width // dp
    chips = tensor // 2
    share = half // chips
    f32, bf16 = jnp.float32, jnp.bfloat16
    w_in_flat = w_in.reshape(width, 3 * chans)
    core = lax.axis_index("tensor") % 2
    place = lax.axis_index("dp")
    along, side = place // 2, place % 2
    is_second = core.astype(f32)
    is_first = 1.0 - is_second

    def to_core(values):
        return lax.ppermute(values, "tensor", [(i, i ^ 1) for i in range(tensor)])

    def to_side(values):
        return lax.ppermute(values, "dp", [(i, i ^ 1) for i in range(dp)])

    def to_line(values, count):
        return lax.ppermute(values, "dp", [(i, (i + 2 * count) % dp) for i in range(dp)])

    def over_chips(values):
        stride = 2
        while stride < tensor:
            there = lax.ppermute(values, "tensor", [(i, i ^ stride) for i in range(tensor)])
            stride *= 2
            if stride < tensor:
                values = values + there
        return values, there

    def mine(values):
        return lax.dynamic_slice_in_dim(values, core * half, half, 0)

    def other(values):
        return lax.dynamic_slice_in_dim(values, (1 - core) * half, half, 0)

    def ordered(own, partner):
        return jnp.concatenate(
            [own * is_first + partner * is_second, own * is_second + partner * is_first], axis=0
        )

    def after(values, *others):
        return lax.optimization_barrier((values, *others))[0]

    def summed(first, second, product):
        sent = product(second)
        own = product(after(first, sent))
        return over_chips(own + to_core(sent))

    chip = lax.axis_index("tensor") // 2

    def spread(quarter):
        return [to_line(quarter, k) for k in range(1, line)]

    def gathered(pieces):
        near = jnp.concatenate(pieces, axis=0)
        stride = 2
        while stride < tensor:
            there = lax.ppermute(near, "tensor", [(i, i ^ stride) for i in range(tensor)])
            stride *= 2
            if stride < tensor:
                near = jnp.concatenate([near, there], axis=0)
        return near, there, to_core(near), to_core(there)

    def conv_forward(tok):
        s1 = lax.rsqrt(jnp.mean(tok * tok, axis=-1, keepdims=True) + eps)
        normed1 = (tok * s1 * norm_first).astype(bf16)
        proj = jnp.dot(normed1, w_in_flat, preferred_element_type=f32)
        gate_b, gate_c, value = (
            proj[:, :chans],
            proj[:, chans : 2 * chans],
            proj[:, 2 * chans :],
        )
        mixed_in = gate_b * value
        conv = (
            conv_taps[0] * shift_down(mixed_in, 2)
            + conv_taps[1] * shift_down(mixed_in, 1)
            + conv_taps[2] * mixed_in
        )
        gated = (gate_c * conv).astype(bf16)
        return s1, normed1, gate_b, gate_c, value, mixed_in, conv, gated

    def conv_backward(d_resid_b, saved):
        _, _, gate_b, gate_c, value, mixed_in, conv, _ = saved
        d_gated = by_transpose(d_resid_b, w_out)
        d_c = d_gated * conv
        d_conv = d_gated * gate_c
        gtaps = jnp.stack(
            [
                jnp.sum(d_conv * shift_down(mixed_in, 2), axis=0),
                jnp.sum(d_conv * shift_down(mixed_in, 1), axis=0),
                jnp.sum(d_conv * mixed_in, axis=0),
            ],
            axis=0,
        )
        d_mixed = (
            conv_taps[2] * d_conv
            + conv_taps[1] * shift_up(d_conv, 1)
            + conv_taps[0] * shift_up(d_conv, 2)
        )
        d_proj = jnp.concatenate([d_mixed * value, d_c, d_mixed * gate_b], axis=1).astype(bf16)
        return d_proj, gtaps

    def ffn(normed2, cot):
        gate_up = jnp.dot(normed2, w_gu_flat, preferred_element_type=f32)
        act, up = gate_up[:, :hid], gate_up[:, hid:]
        sig = jax.nn.sigmoid(act)
        hidden = (act * sig * up).astype(bf16)
        d_hidden = by_transpose(cot, w_down)
        d_act = d_hidden * up * sig * (1.0 + act * (1.0 - sig))
        d_up = d_hidden * act * sig
        return hidden, jnp.concatenate([d_act, d_up], axis=1).astype(bf16)

    xf = tokens.astype(f32)
    saved = conv_forward(xf)
    s1, normed1, gated = saved[0], saved[1], saved[7]
    mix, mix_there = summed(
        mine(gated), other(gated), lambda part: jnp.dot(part, w_out, preferred_element_type=f32)
    )

    cot_quarter = lax.dynamic_slice_in_dim(cotangent, core * half + chip * share, share, 0)
    cot_pieces = spread(cot_quarter.astype(f32))
    w_gu_flat = after(w_gate_up, gated).reshape(width, 2 * hid)
    mix_there, w_gu_flat = lax.optimization_barrier((mix_there, w_gu_flat))
    beside = to_side(after(tokens, gated).astype(f32))

    resid = mine(xf) + (mix + mix_there)
    s2 = lax.rsqrt(jnp.mean(resid * resid, axis=-1, keepdims=True) + eps)
    scaled = resid * s2
    scaled_there = to_core(scaled)
    normed2_pieces = spread(lax.dynamic_slice_in_dim(scaled, chip * share, share, 0))
    cot_far = gathered([after(p, scaled) for p in cot_pieces])
    normed2_near = (jnp.concatenate([scaled, scaled_there], axis=0) * norm_second).astype(
        bf16
    )
    cot_near = jnp.concatenate([mine(cotangent), other(cotangent)], axis=0)
    hidden_near, d_gu_near = ffn(normed2_near, cot_near)
    d_normed2_chip, d_normed2_there = summed(
        d_gu_near[:half], d_gu_near[half:], lambda part: by_transpose(part, w_gu_flat)
    )

    saved_beside = conv_forward(after(beside, d_gu_near))

    d_normed2 = d_normed2_chip + d_normed2_there
    gn2 = jnp.sum(d_normed2 * resid * s2, axis=0)
    weighted2 = d_normed2 * norm_second
    d_resid = (
        mine(cotangent).astype(f32)
        + s2 * weighted2
        - resid * s2**3 * jnp.mean(weighted2 * resid, axis=-1, keepdims=True)
    )
    d_resid_seq = ordered(d_resid, to_core(d_resid)).astype(bf16)
    d_resid_beside = to_side(d_resid)

    d_proj, gtaps = conv_backward(d_resid_seq, saved)
    d_normed1, d_normed1_there = summed(
        mine(d_proj), other(d_proj), lambda part: by_transpose(part, w_in_flat)
    )

    d_resid_beside = after(d_resid_beside, d_proj)
    d_resid_next = ordered(d_resid_beside, to_core(d_resid_beside)).astype(bf16)
    d_proj_beside, _ = conv_backward(d_resid_next, saved_beside)
    both = [
        jnp.concatenate(pair, axis=0)
        for pair in (
            (normed1, saved_beside[1]),
            (d_resid_seq, d_resid_next),
            (d_proj, d_proj_beside),
            (gated, saved_beside[7]),
        )
    ]

    def columns(values, start):
        return lax.dynamic_slice_in_dim(values, start, block, 1)

    def conv_part(k):
        start = (lax.rem(along + k, line) * 2 + side) * block
        grads = jnp.concatenate(
            [cross(columns(both[0], start), both[2]), cross(columns(both[1], start), both[3])],
            axis=1,
        )
        return grads

    parts = [to_line(conv_part(k), k) for k in range(1, line)]
    kept = conv_part(0)
    total = sum(parts, kept)
    grad_in = total[:, : 3 * chans].reshape(block, 3, chans)
    grad_out = total[:, 3 * chans :].T

    normed2_far = gathered([after(p, d_normed2_chip) for p in normed2_pieces])
    gu_here, gu_there, down_here, down_there = far_grads(
        jnp.stack([place, along * 2 + 1 - side]),
        (*normed2_far, *cot_far),
        norm_second.reshape(1, width),
        normed2_near,
        cot_near,
        hidden_near,
        d_gu_near,
        w_gu_flat,
        w_down,
    )
    down_there = to_side(down_there)
    gu_there = to_side(gu_there)
    grad_down = down_here + down_there
    grad_gu = (gu_here + gu_there).swapaxes(0, 1)

    d_normed1 = d_normed1 + d_normed1_there
    xf_mine, s1_mine = mine(xf), mine(s1)
    weighted1 = d_normed1 * norm_first
    grad_mine = (
        d_resid
        + s1_mine * weighted1
        - xf_mine * s1_mine**3 * jnp.mean(weighted1 * xf_mine, axis=-1, keepdims=True)
    )
    grad_tokens = ordered(grad_mine, to_core(grad_mine))

    hidden_late = after(hidden_near, d_proj)
    out, out_there = summed(
        hidden_late[:half],
        hidden_late[half:],
        lambda part: jnp.dot(part, w_down, preferred_element_type=f32),
    )
    out_mine = resid + (out + out_there)
    block_out = ordered(out_mine, to_core(out_mine)).astype(bf16)

    gn1 = jnp.sum(d_normed1 * xf_mine * s1_mine, axis=0)
    gains = jnp.concatenate([gn1, gn2])
    gains = gains + to_core(gains)
    small = jnp.concatenate([gains, gtaps.reshape(-1)])
    small = small + to_side(small)
    stride = 2
    while stride < dp:
        there = lax.ppermute(small, "dp", [(i, i ^ stride) for i in range(dp)])
        small = small + there
        stride *= 2
    return (
        block_out,
        grad_tokens,
        small[:width],
        grad_in,
        small[2 * width : 2 * width + gtaps.size].reshape(gtaps.shape),
        grad_out,
        small[width : 2 * width],
        grad_gu,
        grad_down,
    )


def solution(mesh):
    dp, tensor = mesh.shape["dp"], mesh.shape["tensor"]

    def body(*args):
        if gathers(dp, tensor, *args[0].shape, args[7].shape[0] * tensor):
            return body_gather(dp, tensor, *args)
        return body_scatter(*args)

    return jax.shard_map(
        body,
        mesh=mesh,
        in_specs=(
            P("dp", None),
            P(),
            P(None, None, "tensor"),
            P(None, "tensor"),
            P("tensor", None),
            P(),
            P(None, None, "tensor"),
            P("tensor", None),
            P("dp", None),
        ),
        out_specs=(
            P("dp", None),
            P("dp", None),
            P(),
            P("dp", None, "tensor"),
            P(None, "tensor"),
            P("tensor", "dp"),
            P(),
            P("dp", None, "tensor"),
            P("tensor", "dp"),
        ),
        check_vma=False,
    )
```

```python
import functools

import jax
import jax.numpy as jnp
from jax import lax
from jax.experimental import pallas as pl
from jax.experimental.pallas import tpu as pltpu
from jax.sharding import PartitionSpec as P


eps = 1e-05


def shift_down(values, count):
    pad = jnp.zeros((count, values.shape[1]), values.dtype)
    return jnp.concatenate([pad, values[: values.shape[0] - count]], axis=0)


def shift_up(values, count):
    pad = jnp.zeros((count, values.shape[1]), values.dtype)
    return jnp.concatenate([values[count:], pad], axis=0)


def cross(left, right):
    return lax.dot_general(
        left, right, (((0,), (0,)), ((), ())), preferred_element_type=jnp.float32
    )


def by_transpose(left, right):
    return lax.dot_general(
        left, right, (((1,), (1,)), ((), ())), preferred_element_type=jnp.float32
    )


def body_scatter(tokens, norm_first, w_in, conv_taps, w_out, norm_second, w_gate_up, w_down, cotangent):
    rows, width = tokens.shape
    chans = w_in.shape[2]
    hid = w_down.shape[0]
    w_in_flat = w_in.reshape(width, 3 * chans)
    w_gu_flat = w_gate_up.reshape(width, 2 * hid)
    xf = tokens.astype(jnp.float32)
    s1 = lax.rsqrt(jnp.mean(xf * xf, axis=-1, keepdims=True) + eps)
    normed1 = (xf * s1 * norm_first).astype(jnp.bfloat16)
    proj = jnp.dot(normed1, w_in_flat, preferred_element_type=jnp.float32).reshape(rows, 3, chans)
    gate_b, gate_c, value = (proj[:, 0], proj[:, 1], proj[:, 2])
    mixed_in = gate_b * value
    conv = (
        conv_taps[0] * shift_down(mixed_in, 2)
        + conv_taps[1] * shift_down(mixed_in, 1)
        + conv_taps[2] * mixed_in
    )
    gated = (gate_c * conv).astype(jnp.bfloat16)
    mix = lax.psum(jnp.dot(gated, w_out, preferred_element_type=jnp.float32), "tensor")
    resid = xf + mix
    s2 = lax.rsqrt(jnp.mean(resid * resid, axis=-1, keepdims=True) + eps)
    normed2 = (resid * s2 * norm_second).astype(jnp.bfloat16)
    gate_up = jnp.dot(normed2, w_gu_flat, preferred_element_type=jnp.float32).reshape(rows, 2, hid)
    act, up = (gate_up[:, 0], gate_up[:, 1])
    sig = jax.nn.sigmoid(act)
    hidden = (act * sig * up).astype(jnp.bfloat16)
    ffn = lax.psum(jnp.dot(hidden, w_down, preferred_element_type=jnp.float32), "tensor")
    block_out = (resid + ffn).astype(jnp.bfloat16)
    cotf = cotangent.astype(jnp.float32)
    grad_down = cross(hidden, cotangent)
    d_hidden = by_transpose(cotangent, w_down)
    d_act = d_hidden * up * sig * (1.0 + act * (1.0 - sig))
    d_up = d_hidden * act * sig
    d_gu = jnp.stack([d_act, d_up], axis=1).astype(jnp.bfloat16).reshape(rows, 2 * hid)
    grad_gu = cross(normed2, d_gu).reshape(width, 2, hid)
    d_normed2 = lax.psum(by_transpose(d_gu, w_gu_flat), "tensor")
    gn2 = jnp.sum(d_normed2 * resid * s2, axis=0)
    weighted2 = d_normed2 * norm_second
    d_resid = (
        cotf + s2 * weighted2 - resid * s2**3 * jnp.mean(weighted2 * resid, axis=-1, keepdims=True)
    )
    d_resid_b = d_resid.astype(jnp.bfloat16)
    grad_out = cross(gated, d_resid_b)
    d_gated = by_transpose(d_resid_b, w_out)
    d_c = d_gated * conv
    d_conv = d_gated * gate_c
    gtaps = jnp.stack(
        [
            jnp.sum(d_conv * shift_down(mixed_in, 2), axis=0),
            jnp.sum(d_conv * shift_down(mixed_in, 1), axis=0),
            jnp.sum(d_conv * mixed_in, axis=0),
        ],
        axis=0,
    )
    d_mixed = (
        conv_taps[2] * d_conv
        + conv_taps[1] * shift_up(d_conv, 1)
        + conv_taps[0] * shift_up(d_conv, 2)
    )
    d_proj = (
        jnp.stack([d_mixed * value, d_c, d_mixed * gate_b], axis=1)
        .astype(jnp.bfloat16)
        .reshape(rows, 3 * chans)
    )
    grad_in = cross(normed1, d_proj).reshape(width, 3, chans)
    d_normed1 = lax.psum(by_transpose(d_proj, w_in_flat), "tensor")
    gn1 = jnp.sum(d_normed1 * xf * s1, axis=0)
    weighted1 = d_normed1 * norm_first
    grad_tokens = (
        d_resid + s1 * weighted1 - xf * s1**3 * jnp.mean(weighted1 * xf, axis=-1, keepdims=True)
    )
    shared_in, shared_out, shared_gu, shared_down = (
        lax.psum_scatter(grad_in, "dp", scatter_dimension=0, tiled=True),
        lax.psum_scatter(grad_out, "dp", scatter_dimension=1, tiled=True),
        lax.psum_scatter(grad_gu, "dp", scatter_dimension=0, tiled=True),
        lax.psum_scatter(grad_down, "dp", scatter_dimension=1, tiled=True),
    )
    sum_taps, sum_n1, sum_n2 = lax.psum((gtaps, gn1, gn2), "dp")
    return (
        block_out,
        grad_tokens,
        sum_n1,
        shared_in,
        sum_taps,
        shared_out,
        sum_n2,
        shared_gu,
        shared_down,
    )


def gathers(dp, tensor, rows, width, hid):
    powers = tensor == 4 and dp > 2 and dp & (dp - 1) == 0
    whole = rows % (8 * tensor) == 0 and hid % (128 * tensor) == 0
    return powers and whole and width % (128 * dp) == 0 and dp * rows <= 2 * width


def join_kernel(*refs):
    start = 0
    for ref in refs[:-1]:
        refs[-1][start : start + ref.shape[0]] = ref[...]
        start += ref.shape[0]


def join(pieces):
    rows = sum(piece.shape[0] for piece in pieces)
    return pl.pallas_call(
        join_kernel,
        out_shape=jax.ShapeDtypeStruct((rows, *pieces[0].shape[1:]), pieces[0].dtype),
        compiler_params=pltpu.CompilerParams(vmem_limit_bytes=4 << 20),
        cost_estimate=pl.CostEstimate(
            flops=0, bytes_accessed=2 * rows * pieces[0].shape[1] * 4, transcendentals=0
        ),
        name="join",
    )(*pieces)


def conv_kernel(at_block, *refs, block):
    first, second, refs = refs[:4], refs[4:8], refs[8:]
    for k, out in enumerate(refs):
        at = pl.ds(pl.multiple_of(at_block[k] * block, block), block)
        split = first[2].shape[1]
        out[:, :split] = cross(first[0][:, at], first[2][...]) + cross(
            second[0][:, at], second[2][...]
        )
        out[:, split:] = cross(first[1][:, at], first[3][...]) + cross(
            second[1][:, at], second[3][...]
        )


def conv_parts(at_block, first, second, line, block):
    rows, chans = first[3].shape
    return pl.pallas_call(
        functools.partial(conv_kernel, block=block),
        out_shape=[jax.ShapeDtypeStruct((block, 4 * chans), jnp.float32)] * line,
        grid_spec=pltpu.PrefetchScalarGridSpec(
            num_scalar_prefetch=1,
            grid=(),
            in_specs=[pl.BlockSpec(memory_space=pltpu.VMEM)] * 8,
            out_specs=[pl.BlockSpec(memory_space=pltpu.VMEM)] * line,
        ),
        compiler_params=pltpu.CompilerParams(vmem_limit_bytes=16 << 20),
        cost_estimate=pl.CostEstimate(
            flops=16 * rows * line * block * chans,
            bytes_accessed=16 * rows * (line * 2 * block + 2 * chans),
            transcendentals=0,
        ),
        name="conv_parts",
    )(at_block, *first, *second)


def far_kernel(
    where,
    *refs,
    rows,
    share,
    block,
):
    normed, cots, refs = refs[:4], refs[4:8], refs[8:]
    norm, x_near, c_near, h_near, dg_near, du_near, wg, wu, wd = refs[:9]
    gu_own, gu_there, down_own, down_there = refs[9:13]
    x_all, c_all, xs, cs, w_both, d_both, hidden = refs[13:]
    step = wd.shape[0]
    f32, bf16 = jnp.float32, jnp.bfloat16

    @pl.when(pl.program_id(0) == 0)
    def _():
        x_all[:rows] = x_near[...]
        c_all[:rows] = c_near[...]
        for i in range(4):
            at = pl.ds(rows + i * share, share)
            x_all[at] = (normed[i][...] * norm[...]).astype(bf16)
            c_all[at] = cots[i][...].astype(bf16)
        for i in range(2):
            at = pl.ds(pl.multiple_of(where[i] * block, block), block)
            xs[:, i * block : (i + 1) * block] = x_all[:, at]
            cs[:, i * block : (i + 1) * block] = c_all[:, at]

    w_both[:, :step] = wg[...]
    w_both[:, step:] = wu[...]
    hidden[:rows] = h_near[...]
    d_both[:rows, :step] = dg_near[...]
    d_both[:rows, step:] = du_near[...]
    acts = jnp.dot(x_all[rows:], w_both[...], preferred_element_type=f32)
    act, up = acts[:, :step], acts[:, step:]
    d_hidden = by_transpose(c_all[rows:], wd[...])
    sig = jax.nn.sigmoid(act)
    product = act * sig
    hidden[rows:] = (product * up).astype(bf16)
    d_both[rows:, :step] = (d_hidden * up * sig * (1.0 + act * (1.0 - sig))).astype(bf16)
    d_both[rows:, step:] = (d_hidden * product).astype(bf16)
    both = cross(xs[...], d_both[...])
    for i in range(2):
        gu_own[i] = both[:block, i * step : (i + 1) * step]
        gu_there[i] = both[block:, i * step : (i + 1) * step]
    both = cross(hidden[...], cs[...])
    down_own[...] = both[:, :block]
    down_there[...] = both[:, block:]


def far_grads(where, block, normed, cots, norm, x_near, c_near, h_near, d_gu_near, w_gu, w_down):
    rows, width = x_near.shape
    hid = w_down.shape[0]
    share = normed[0].shape[0]
    tokens = rows + 4 * share
    step = max(size for size in range(128, 513, 128) if hid % size == 0)
    steps = hid // step
    f32, bf16 = jnp.float32, jnp.bfloat16

    def whole(array):
        return pl.BlockSpec(
            array.shape, lambda j, _: (0,) * array.ndim, pipeline_mode=pl.Buffered(1)
        )

    return pl.pallas_call(
        functools.partial(far_kernel, rows=rows, share=share, block=block),
        out_shape=(
            *[jax.ShapeDtypeStruct((2, block, hid), f32)] * 2,
            *[jax.ShapeDtypeStruct((hid, block), f32)] * 2,
        ),
        grid_spec=pltpu.PrefetchScalarGridSpec(
            num_scalar_prefetch=1,
            grid=(steps,),
            in_specs=[
                *[whole(piece) for piece in (*normed, *cots)],
                whole(norm),
                whole(x_near),
                whole(c_near),
                pl.BlockSpec((rows, step), lambda j, _: (0, j)),
                pl.BlockSpec((rows, step), lambda j, _: (0, j)),
                pl.BlockSpec((rows, step), lambda j, _: (0, j + steps)),
                pl.BlockSpec((width, step), lambda j, _: (0, j)),
                pl.BlockSpec((width, step), lambda j, _: (0, j + steps)),
                pl.BlockSpec((step, width), lambda j, _: (j, 0)),
            ],
            out_specs=[
                *[pl.BlockSpec((2, block, step), lambda j, _: (0, 0, j))] * 2,
                *[pl.BlockSpec((step, block), lambda j, _: (j, 0))] * 2,
            ],
            scratch_shapes=[
                *[pltpu.VMEM((tokens, width), bf16)] * 2,
                *[pltpu.VMEM((tokens, 2 * block), bf16)] * 2,
                pltpu.VMEM((width, 2 * step), bf16),
                pltpu.VMEM((tokens, 2 * step), bf16),
                pltpu.VMEM((tokens, step), bf16),
            ],
        ),
        compiler_params=pltpu.CompilerParams(vmem_limit_bytes=52 << 20),
        cost_estimate=pl.CostEstimate(
            flops=6 * hid * (tokens - rows) * width + 12 * hid * tokens * block,
            bytes_accessed=8 * (tokens - rows) * width + 6 * hid * width + 24 * hid * block,
            transcendentals=(tokens - rows) * hid,
        ),
        name="far_grads",
    )(where, *normed, *cots, norm, x_near, c_near, h_near, d_gu_near, d_gu_near, w_gu, w_gu, w_down)


def body_gather(
    dp,
    tensor,
    tokens,
    norm_first,
    w_in,
    conv_taps,
    w_out,
    norm_second,
    w_gate_up,
    w_down,
    cotangent,
):
    rows, width = tokens.shape
    chans = w_in.shape[2]
    hid = w_down.shape[0]
    half = rows // 2
    line = dp // 2
    block = width // dp
    chips = tensor // 2
    share = half // chips
    f32, bf16 = jnp.float32, jnp.bfloat16
    w_in_flat = w_in.reshape(width, 3 * chans)
    core = lax.axis_index("tensor") % 2
    place = lax.axis_index("dp")
    along, side = place // 2, place % 2
    is_second = core.astype(f32)
    is_first = 1.0 - is_second

    def to_core(values):
        return lax.ppermute(values, "tensor", [(i, i ^ 1) for i in range(tensor)])

    def to_side(values):
        return lax.ppermute(values, "dp", [(i, i ^ 1) for i in range(dp)])

    def to_line(values, count):
        return lax.ppermute(values, "dp", [(i, (i + 2 * count) % dp) for i in range(dp)])

    def over_chips(values):
        stride = 2
        while stride < tensor:
            there = lax.ppermute(values, "tensor", [(i, i ^ stride) for i in range(tensor)])
            stride *= 2
            if stride < tensor:
                values = values + there
        return values, there

    def mine(values):
        return lax.dynamic_slice_in_dim(values, core * half, half, 0)

    def other(values):
        return lax.dynamic_slice_in_dim(values, (1 - core) * half, half, 0)

    def ordered(own, partner):
        return jnp.concatenate(
            [own * is_first + partner * is_second, own * is_second + partner * is_first], axis=0
        )

    def after(values, *others):
        return lax.optimization_barrier((values, *others))[0]

    def summed(first, second, product):
        sent = product(second)
        own = product(after(first, sent))
        return over_chips(own + to_core(sent))

    chip = lax.axis_index("tensor") // 2

    def along_line(values):
        return [to_line(values, k) for k in range(1, line)]

    def quarter(values, start):
        return lax.dynamic_slice_in_dim(values, start + chip * share, share, 0)

    def gathered(pieces):
        near = join(pieces)
        there = lax.ppermute(near, "tensor", [(i, i ^ 2) for i in range(tensor)])
        return near, there, to_core(near), to_core(there)

    def conv_forward(tok):
        s1 = lax.rsqrt(jnp.mean(tok * tok, axis=-1, keepdims=True) + eps)
        normed1 = (tok * s1 * norm_first).astype(bf16)
        proj = jnp.dot(normed1, w_in_flat, preferred_element_type=f32)
        gate_b, gate_c, value = (
            proj[:, :chans],
            proj[:, chans : 2 * chans],
            proj[:, 2 * chans :],
        )
        mixed_in = gate_b * value
        conv = (
            conv_taps[0] * shift_down(mixed_in, 2)
            + conv_taps[1] * shift_down(mixed_in, 1)
            + conv_taps[2] * mixed_in
        )
        gated = (gate_c * conv).astype(bf16)
        return s1, normed1, gate_b, gate_c, value, mixed_in, conv, gated

    def conv_backward(d_resid_b, saved):
        _, _, gate_b, gate_c, value, mixed_in, conv, _ = saved
        d_gated = by_transpose(d_resid_b, w_out)
        d_c = d_gated * conv
        d_conv = d_gated * gate_c
        gtaps = jnp.stack(
            [
                jnp.sum(d_conv * shift_down(mixed_in, 2), axis=0),
                jnp.sum(d_conv * shift_down(mixed_in, 1), axis=0),
                jnp.sum(d_conv * mixed_in, axis=0),
            ],
            axis=0,
        )
        d_mixed = (
            conv_taps[2] * d_conv
            + conv_taps[1] * shift_up(d_conv, 1)
            + conv_taps[0] * shift_up(d_conv, 2)
        )
        d_proj = jnp.concatenate([d_mixed * value, d_c, d_mixed * gate_b], axis=1).astype(bf16)
        return d_proj, gtaps

    def ffn(normed2, cot):
        gate_up = jnp.dot(normed2, w_gu_flat, preferred_element_type=f32)
        act, up = gate_up[:, :hid], gate_up[:, hid:]
        sig = jax.nn.sigmoid(act)
        hidden = (act * sig * up).astype(bf16)
        d_hidden = by_transpose(cot, w_down)
        d_act = d_hidden * up * sig * (1.0 + act * (1.0 - sig))
        d_up = d_hidden * act * sig
        return hidden, jnp.concatenate([d_act, d_up], axis=1).astype(bf16)

    xf = tokens.astype(f32)
    saved = conv_forward(xf)
    s1, normed1, gated = saved[0], saved[1], saved[7]
    mix, mix_there = summed(
        mine(gated), other(gated), lambda part: jnp.dot(part, w_out, preferred_element_type=f32)
    )

    cot_pieces = along_line(quarter(cotangent, core * half).astype(f32))
    w_gu_flat = after(w_gate_up, gated).reshape(width, 2 * hid)
    mix_there, w_gu_flat = lax.optimization_barrier((mix_there, w_gu_flat))
    beside = to_side(after(tokens, gated).astype(f32))

    resid = mine(xf) + (mix + mix_there)
    s2 = lax.rsqrt(jnp.mean(resid * resid, axis=-1, keepdims=True) + eps)
    scaled = resid * s2
    scaled_there = to_core(scaled)
    normed2_pieces = along_line(quarter(scaled, 0))
    cot_far = gathered([after(piece, scaled) for piece in cot_pieces])
    normed2_near = (jnp.concatenate([scaled, scaled_there], axis=0) * norm_second).astype(
        bf16
    )
    cot_near = jnp.concatenate([mine(cotangent), other(cotangent)], axis=0)
    hidden_near, d_gu_near = ffn(normed2_near, cot_near)
    d_normed2_chip, d_normed2_there = summed(
        d_gu_near[:half], d_gu_near[half:], lambda part: by_transpose(part, w_gu_flat)
    )

    saved_beside = conv_forward(after(beside, d_gu_near))

    d_normed2 = d_normed2_chip + d_normed2_there
    gn2 = jnp.sum(d_normed2 * resid * s2, axis=0)
    weighted2 = d_normed2 * norm_second
    d_resid = (
        mine(cotangent).astype(f32)
        + s2 * weighted2
        - resid * s2**3 * jnp.mean(weighted2 * resid, axis=-1, keepdims=True)
    )
    d_resid_seq = ordered(d_resid, to_core(d_resid)).astype(bf16)
    d_resid_beside = to_side(d_resid)

    d_proj, gtaps = conv_backward(d_resid_seq, saved)
    d_normed1, d_normed1_there = summed(
        mine(d_proj), other(d_proj), lambda part: by_transpose(part, w_in_flat)
    )

    d_resid_beside = after(d_resid_beside, d_proj)
    d_resid_next = ordered(d_resid_beside, to_core(d_resid_beside)).astype(bf16)
    d_proj_beside, _ = conv_backward(d_resid_next, saved_beside)

    kept, *parts = conv_parts(
        lax.rem(along + jnp.arange(line, dtype=jnp.int32), line) * 2 + side,
        (normed1, d_resid_seq, d_proj, gated),
        (saved_beside[1], d_resid_next, d_proj_beside, saved_beside[7]),
        line,
        block,
    )
    parts = [to_line(part, k + 1) for k, part in enumerate(parts)]
    total = sum(parts, kept)
    grad_in = total[:, : 3 * chans].reshape(block, 3, chans)
    grad_out = total[:, 3 * chans :].T

    normed2_far = gathered([after(piece, d_resid) for piece in normed2_pieces])
    gu_here, gu_there, down_here, down_there = far_grads(
        jnp.stack([place, along * 2 + 1 - side]),
        block,
        normed2_far,
        cot_far,
        norm_second.reshape(1, width),
        normed2_near,
        cot_near,
        hidden_near,
        d_gu_near,
        w_gu_flat,
        w_down,
    )
    gu_there = to_side(gu_there)
    down_there = to_side(down_there)
    grad_gu = (gu_here + gu_there).swapaxes(0, 1)
    grad_down = down_here + down_there

    d_normed1 = d_normed1 + d_normed1_there
    xf_mine, s1_mine = mine(xf), mine(s1)
    weighted1 = d_normed1 * norm_first
    grad_mine = (
        d_resid
        + s1_mine * weighted1
        - xf_mine * s1_mine**3 * jnp.mean(weighted1 * xf_mine, axis=-1, keepdims=True)
    )
    grad_tokens = ordered(grad_mine, to_core(grad_mine))

    hidden_late = after(hidden_near, d_proj)
    out, out_there = summed(
        hidden_late[:half],
        hidden_late[half:],
        lambda part: jnp.dot(part, w_down, preferred_element_type=f32),
    )
    out_mine = resid + (out + out_there)
    block_out = ordered(out_mine, to_core(out_mine)).astype(bf16)

    gn1 = jnp.sum(d_normed1 * xf_mine * s1_mine, axis=0)
    gains = jnp.concatenate([gn1, gn2])
    gains = gains + to_core(gains)
    small = jnp.concatenate([gains, gtaps.reshape(-1)])
    stride = 2
    while stride < dp:
        there = lax.ppermute(small, "dp", [(i, i ^ stride) for i in range(dp)])
        small = small + there
        stride *= 2
    small = small + to_side(small)
    return (
        block_out,
        grad_tokens,
        small[:width],
        grad_in,
        small[2 * width : 2 * width + gtaps.size].reshape(gtaps.shape),
        grad_out,
        small[width : 2 * width],
        grad_gu,
        grad_down,
    )


def solution(mesh):
    dp, tensor = mesh.shape["dp"], mesh.shape["tensor"]

    def body(*args):
        if gathers(dp, tensor, *args[0].shape, args[7].shape[0] * tensor):
            return body_gather(dp, tensor, *args)
        return body_scatter(*args)

    return jax.shard_map(
        body,
        mesh=mesh,
        in_specs=(
            P("dp", None),
            P(),
            P(None, None, "tensor"),
            P(None, "tensor"),
            P("tensor", None),
            P(),
            P(None, None, "tensor"),
            P("tensor", None),
            P("dp", None),
        ),
        out_specs=(
            P("dp", None),
            P("dp", None),
            P(),
            P("dp", None, "tensor"),
            P(None, "tensor"),
            P("tensor", "dp"),
            P(),
            P("dp", None, "tensor"),
            P("tensor", "dp"),
        ),
        check_vma=False,
    )
```

```python
import functools

import jax
import jax.numpy as jnp
from jax import lax
from jax.experimental import pallas as pl
from jax.experimental.pallas import tpu as pltpu
from jax.sharding import PartitionSpec as P


eps = 1e-05


def shift_down(values, count):
    pad = jnp.zeros((count, values.shape[1]), values.dtype)
    return jnp.concatenate([pad, values[: values.shape[0] - count]], axis=0)


def shift_up(values, count):
    pad = jnp.zeros((count, values.shape[1]), values.dtype)
    return jnp.concatenate([values[count:], pad], axis=0)


def cross(left, right):
    return lax.dot_general(
        left, right, (((0,), (0,)), ((), ())), preferred_element_type=jnp.float32
    )


def by_transpose(left, right):
    return lax.dot_general(
        left, right, (((1,), (1,)), ((), ())), preferred_element_type=jnp.float32
    )


def body_scatter(tokens, norm_first, w_in, conv_taps, w_out, norm_second, w_gate_up, w_down, cotangent):
    rows, width = tokens.shape
    chans = w_in.shape[2]
    hid = w_down.shape[0]
    w_in_flat = w_in.reshape(width, 3 * chans)
    w_gu_flat = w_gate_up.reshape(width, 2 * hid)
    xf = tokens.astype(jnp.float32)
    s1 = lax.rsqrt(jnp.mean(xf * xf, axis=-1, keepdims=True) + eps)
    normed1 = (xf * s1 * norm_first).astype(jnp.bfloat16)
    proj = jnp.dot(normed1, w_in_flat, preferred_element_type=jnp.float32).reshape(rows, 3, chans)
    gate_b, gate_c, value = (proj[:, 0], proj[:, 1], proj[:, 2])
    mixed_in = gate_b * value
    conv = (
        conv_taps[0] * shift_down(mixed_in, 2)
        + conv_taps[1] * shift_down(mixed_in, 1)
        + conv_taps[2] * mixed_in
    )
    gated = (gate_c * conv).astype(jnp.bfloat16)
    mix = lax.psum(jnp.dot(gated, w_out, preferred_element_type=jnp.float32), "tensor")
    resid = xf + mix
    s2 = lax.rsqrt(jnp.mean(resid * resid, axis=-1, keepdims=True) + eps)
    normed2 = (resid * s2 * norm_second).astype(jnp.bfloat16)
    gate_up = jnp.dot(normed2, w_gu_flat, preferred_element_type=jnp.float32).reshape(rows, 2, hid)
    act, up = (gate_up[:, 0], gate_up[:, 1])
    sig = jax.nn.sigmoid(act)
    hidden = (act * sig * up).astype(jnp.bfloat16)
    ffn = lax.psum(jnp.dot(hidden, w_down, preferred_element_type=jnp.float32), "tensor")
    block_out = (resid + ffn).astype(jnp.bfloat16)
    cotf = cotangent.astype(jnp.float32)
    grad_down = cross(hidden, cotangent)
    d_hidden = by_transpose(cotangent, w_down)
    d_act = d_hidden * up * sig * (1.0 + act * (1.0 - sig))
    d_up = d_hidden * act * sig
    d_gu = jnp.stack([d_act, d_up], axis=1).astype(jnp.bfloat16).reshape(rows, 2 * hid)
    grad_gu = cross(normed2, d_gu).reshape(width, 2, hid)
    d_normed2 = lax.psum(by_transpose(d_gu, w_gu_flat), "tensor")
    gn2 = jnp.sum(d_normed2 * resid * s2, axis=0)
    weighted2 = d_normed2 * norm_second
    d_resid = (
        cotf + s2 * weighted2 - resid * s2**3 * jnp.mean(weighted2 * resid, axis=-1, keepdims=True)
    )
    d_resid_b = d_resid.astype(jnp.bfloat16)
    grad_out = cross(gated, d_resid_b)
    d_gated = by_transpose(d_resid_b, w_out)
    d_c = d_gated * conv
    d_conv = d_gated * gate_c
    gtaps = jnp.stack(
        [
            jnp.sum(d_conv * shift_down(mixed_in, 2), axis=0),
            jnp.sum(d_conv * shift_down(mixed_in, 1), axis=0),
            jnp.sum(d_conv * mixed_in, axis=0),
        ],
        axis=0,
    )
    d_mixed = (
        conv_taps[2] * d_conv
        + conv_taps[1] * shift_up(d_conv, 1)
        + conv_taps[0] * shift_up(d_conv, 2)
    )
    d_proj = (
        jnp.stack([d_mixed * value, d_c, d_mixed * gate_b], axis=1)
        .astype(jnp.bfloat16)
        .reshape(rows, 3 * chans)
    )
    grad_in = cross(normed1, d_proj).reshape(width, 3, chans)
    d_normed1 = lax.psum(by_transpose(d_proj, w_in_flat), "tensor")
    gn1 = jnp.sum(d_normed1 * xf * s1, axis=0)
    weighted1 = d_normed1 * norm_first
    grad_tokens = (
        d_resid + s1 * weighted1 - xf * s1**3 * jnp.mean(weighted1 * xf, axis=-1, keepdims=True)
    )
    shared_in, shared_out, shared_gu, shared_down = (
        lax.psum_scatter(grad_in, "dp", scatter_dimension=0, tiled=True),
        lax.psum_scatter(grad_out, "dp", scatter_dimension=1, tiled=True),
        lax.psum_scatter(grad_gu, "dp", scatter_dimension=0, tiled=True),
        lax.psum_scatter(grad_down, "dp", scatter_dimension=1, tiled=True),
    )
    sum_taps, sum_n1, sum_n2 = lax.psum((gtaps, gn1, gn2), "dp")
    return (
        block_out,
        grad_tokens,
        sum_n1,
        shared_in,
        sum_taps,
        shared_out,
        sum_n2,
        shared_gu,
        shared_down,
    )


def gathers(dp, tensor, rows, width, hid):
    powers = tensor == 4 and dp > 2 and dp & (dp - 1) == 0
    whole = rows % (8 * tensor) == 0 and hid % (128 * tensor) == 0
    whole = whole and (hid // tensor % 256 == 0 or hid // tensor % 384 == 0)
    return powers and whole and width % (128 * dp) == 0 and dp * rows <= 2 * width


def join_kernel(*refs):
    start = 0
    for ref in refs[:-1]:
        refs[-1][start : start + ref.shape[0]] = ref[...]
        start += ref.shape[0]


def join(pieces):
    rows = sum(piece.shape[0] for piece in pieces)
    return pl.pallas_call(
        join_kernel,
        out_shape=jax.ShapeDtypeStruct((rows, *pieces[0].shape[1:]), pieces[0].dtype),
        compiler_params=pltpu.CompilerParams(vmem_limit_bytes=4 << 20),
        cost_estimate=pl.CostEstimate(
            flops=0, bytes_accessed=2 * rows * pieces[0].shape[1] * 4, transcendentals=0
        ),
        name="join",
    )(*pieces)


def conv_kernel(at_block, *refs, block):
    first, second, refs = refs[:4], refs[4:8], refs[8:]
    for k, out in enumerate(refs):
        at = pl.ds(pl.multiple_of(at_block[k] * block, block), block)
        split = first[2].shape[1]
        out[:, :split] = cross(first[0][:, at], first[2][...]) + cross(
            second[0][:, at], second[2][...]
        )
        out[:, split:] = cross(first[1][:, at], first[3][...]) + cross(
            second[1][:, at], second[3][...]
        )


def conv_parts(at_block, first, second, line, block):
    rows, chans = first[3].shape
    return pl.pallas_call(
        functools.partial(conv_kernel, block=block),
        out_shape=[jax.ShapeDtypeStruct((block, 4 * chans), jnp.float32)] * line,
        grid_spec=pltpu.PrefetchScalarGridSpec(
            num_scalar_prefetch=1,
            grid=(),
            in_specs=[pl.BlockSpec(memory_space=pltpu.VMEM)] * 8,
            out_specs=[pl.BlockSpec(memory_space=pltpu.VMEM)] * line,
        ),
        compiler_params=pltpu.CompilerParams(vmem_limit_bytes=16 << 20),
        cost_estimate=pl.CostEstimate(
            flops=16 * rows * line * block * chans,
            bytes_accessed=16 * rows * (line * 2 * block + 2 * chans),
            transcendentals=0,
        ),
        name="conv_parts",
    )(at_block, *first, *second)


def far_kernel(
    where,
    *refs,
    rows,
    share,
    block,
):
    normed, cots, refs = refs[:4], refs[4:8], refs[8:]
    norm, x_near, c_near, h_near, dg_near, du_near, wg, wu, wd = refs[:9]
    gu_own, gu_there, down_own, down_there = refs[9:13]
    x_all, c_all, xs, cs, w_both, d_both, hidden = refs[13:]
    step = wd.shape[0]
    f32, bf16 = jnp.float32, jnp.bfloat16

    @pl.when(pl.program_id(0) == 0)
    def _():
        x_all[:rows] = x_near[...]
        c_all[:rows] = c_near[...]
        for i in range(4):
            at = pl.ds(rows + i * share, share)
            x_all[at] = (normed[i][...] * norm[...]).astype(bf16)
            c_all[at] = cots[i][...].astype(bf16)
        for i in range(2):
            at = pl.ds(pl.multiple_of(where[i] * block, block), block)
            xs[:, i * block : (i + 1) * block] = x_all[:, at]
            cs[:, i * block : (i + 1) * block] = c_all[:, at]

    w_both[:, :step] = wg[...]
    w_both[:, step:] = wu[...]
    hidden[:rows] = h_near[...]
    d_both[:rows, :step] = dg_near[...]
    d_both[:rows, step:] = du_near[...]
    acts = jnp.dot(x_all[rows:], w_both[...], preferred_element_type=f32)
    act, up = acts[:, :step], acts[:, step:]
    d_hidden = by_transpose(c_all[rows:], wd[...])
    sig = jax.nn.sigmoid(act)
    product = act * sig
    hidden[rows:] = (product * up).astype(bf16)
    d_both[rows:, :step] = (d_hidden * up * sig * (1.0 + act * (1.0 - sig))).astype(bf16)
    d_both[rows:, step:] = (d_hidden * product).astype(bf16)
    both = cross(xs[...], d_both[...])
    for i in range(2):
        gu_own[i] = both[:block, i * step : (i + 1) * step]
        gu_there[i] = both[block:, i * step : (i + 1) * step]
    both = cross(hidden[...], cs[...])
    down_own[...] = both[:, :block]
    down_there[...] = both[:, block:]


def far_grads(where, block, piece, normed, cots, norm, x_near, c_near, h_near, d_gu_near, w_gu, w_down):
    rows, width = x_near.shape
    hid = w_down.shape[0]
    share = normed[0].shape[0]
    tokens = rows + 4 * share
    step = max(size for size in range(128, 513, 128) if hid % size == 0)
    all_steps = hid // step
    early = max(1, all_steps // 3)
    start, steps = ((0, early), (early, all_steps - early))[piece]
    hid = steps * step
    f32, bf16 = jnp.float32, jnp.bfloat16

    def whole(array):
        return pl.BlockSpec(
            array.shape, lambda j, _: (0,) * array.ndim, pipeline_mode=pl.Buffered(1)
        )

    return pl.pallas_call(
        functools.partial(far_kernel, rows=rows, share=share, block=block),
        out_shape=(
            *[jax.ShapeDtypeStruct((2, block, hid), f32)] * 2,
            *[jax.ShapeDtypeStruct((hid, block), f32)] * 2,
        ),
        grid_spec=pltpu.PrefetchScalarGridSpec(
            num_scalar_prefetch=1,
            grid=(steps,),
            in_specs=[
                *[whole(piece) for piece in (*normed, *cots)],
                whole(norm),
                whole(x_near),
                whole(c_near),
                pl.BlockSpec((rows, step), lambda j, _: (0, j + start)),
                pl.BlockSpec((rows, step), lambda j, _: (0, j + start)),
                pl.BlockSpec((rows, step), lambda j, _: (0, j + start + all_steps)),
                pl.BlockSpec((width, step), lambda j, _: (0, j + start)),
                pl.BlockSpec((width, step), lambda j, _: (0, j + start + all_steps)),
                pl.BlockSpec((step, width), lambda j, _: (j + start, 0)),
            ],
            out_specs=[
                *[pl.BlockSpec((2, block, step), lambda j, _: (0, 0, j))] * 2,
                *[pl.BlockSpec((step, block), lambda j, _: (j, 0))] * 2,
            ],
            scratch_shapes=[
                *[pltpu.VMEM((tokens, width), bf16)] * 2,
                *[pltpu.VMEM((tokens, 2 * block), bf16)] * 2,
                pltpu.VMEM((width, 2 * step), bf16),
                pltpu.VMEM((tokens, 2 * step), bf16),
                pltpu.VMEM((tokens, step), bf16),
            ],
        ),
        compiler_params=pltpu.CompilerParams(vmem_limit_bytes=52 << 20),
        cost_estimate=pl.CostEstimate(
            flops=6 * hid * (tokens - rows) * width + 12 * hid * tokens * block,
            bytes_accessed=8 * (tokens - rows) * width + 6 * hid * width + 24 * hid * block,
            transcendentals=(tokens - rows) * hid,
        ),
    )(where, *normed, *cots, norm, x_near, c_near, h_near, d_gu_near, d_gu_near, w_gu, w_gu, w_down)


def body_gather(
    dp,
    tensor,
    tokens,
    norm_first,
    w_in,
    conv_taps,
    w_out,
    norm_second,
    w_gate_up,
    w_down,
    cotangent,
):
    rows, width = tokens.shape
    chans = w_in.shape[2]
    hid = w_down.shape[0]
    half = rows // 2
    line = dp // 2
    block = width // dp
    chips = tensor // 2
    share = half // chips
    f32, bf16 = jnp.float32, jnp.bfloat16
    w_in_flat = w_in.reshape(width, 3 * chans)
    core = lax.axis_index("tensor") % 2
    place = lax.axis_index("dp")
    along, side = place // 2, place % 2
    is_second = core.astype(f32)
    is_first = 1.0 - is_second

    def to_core(values):
        return lax.ppermute(values, "tensor", [(i, i ^ 1) for i in range(tensor)])

    def to_side(values):
        return lax.ppermute(values, "dp", [(i, i ^ 1) for i in range(dp)])

    def to_line(values, count):
        return lax.ppermute(values, "dp", [(i, (i + 2 * count) % dp) for i in range(dp)])

    def over_chips(values):
        stride = 2
        while stride < tensor:
            there = lax.ppermute(values, "tensor", [(i, i ^ stride) for i in range(tensor)])
            stride *= 2
            if stride < tensor:
                values = values + there
        return values, there

    def mine(values):
        return lax.dynamic_slice_in_dim(values, core * half, half, 0)

    def other(values):
        return lax.dynamic_slice_in_dim(values, (1 - core) * half, half, 0)

    def ordered(own, partner):
        return jnp.concatenate(
            [own * is_first + partner * is_second, own * is_second + partner * is_first], axis=0
        )

    def after(values, *others):
        return lax.optimization_barrier((values, *others))[0]

    def summed(first, second, product):
        sent = product(second)
        own = product(after(first, sent))
        return over_chips(own + to_core(sent))

    chip = lax.axis_index("tensor") // 2

    def along_line(values):
        return [to_line(values, k) for k in range(1, line)]

    def quarter(values, start):
        return lax.dynamic_slice_in_dim(values, start + chip * share, share, 0)

    def gathered(pieces):
        near = join(pieces)
        there = lax.ppermute(near, "tensor", [(i, i ^ 2) for i in range(tensor)])
        return near, there, to_core(near), to_core(there)

    def conv_forward(tok):
        s1 = lax.rsqrt(jnp.mean(tok * tok, axis=-1, keepdims=True) + eps)
        normed1 = (tok * s1 * norm_first).astype(bf16)
        proj = jnp.dot(normed1, w_in_flat, preferred_element_type=f32)
        gate_b, gate_c, value = (
            proj[:, :chans],
            proj[:, chans : 2 * chans],
            proj[:, 2 * chans :],
        )
        mixed_in = gate_b * value
        conv = (
            conv_taps[0] * shift_down(mixed_in, 2)
            + conv_taps[1] * shift_down(mixed_in, 1)
            + conv_taps[2] * mixed_in
        )
        gated = (gate_c * conv).astype(bf16)
        return s1, normed1, gate_b, gate_c, value, mixed_in, conv, gated

    def conv_backward(d_resid_b, saved):
        _, _, gate_b, gate_c, value, mixed_in, conv, _ = saved
        d_gated = by_transpose(d_resid_b, w_out)
        d_c = d_gated * conv
        d_conv = d_gated * gate_c
        gtaps = jnp.stack(
            [
                jnp.sum(d_conv * shift_down(mixed_in, 2), axis=0),
                jnp.sum(d_conv * shift_down(mixed_in, 1), axis=0),
                jnp.sum(d_conv * mixed_in, axis=0),
            ],
            axis=0,
        )
        d_mixed = (
            conv_taps[2] * d_conv
            + conv_taps[1] * shift_up(d_conv, 1)
            + conv_taps[0] * shift_up(d_conv, 2)
        )
        d_proj = jnp.concatenate([d_mixed * value, d_c, d_mixed * gate_b], axis=1).astype(bf16)
        return d_proj, gtaps

    def ffn(normed2, cot):
        gate_up = jnp.dot(normed2, w_gu_flat, preferred_element_type=f32)
        act, up = gate_up[:, :hid], gate_up[:, hid:]
        sig = jax.nn.sigmoid(act)
        hidden = (act * sig * up).astype(bf16)
        d_hidden = by_transpose(cot, w_down)
        d_act = d_hidden * up * sig * (1.0 + act * (1.0 - sig))
        d_up = d_hidden * act * sig
        return hidden, jnp.concatenate([d_act, d_up], axis=1).astype(bf16)

    xf = tokens.astype(f32)
    saved = conv_forward(xf)
    s1, normed1, gated = saved[0], saved[1], saved[7]
    mix, mix_there = summed(
        mine(gated), other(gated), lambda part: jnp.dot(part, w_out, preferred_element_type=f32)
    )

    cot_pieces = along_line(quarter(cotangent, core * half).astype(f32))
    w_gu_flat = after(w_gate_up, gated).reshape(width, 2 * hid)
    mix_there, w_gu_flat = lax.optimization_barrier((mix_there, w_gu_flat))
    beside = to_side(after(tokens, gated).astype(f32))

    resid = mine(xf) + (mix + mix_there)
    s2 = lax.rsqrt(jnp.mean(resid * resid, axis=-1, keepdims=True) + eps)
    scaled = resid * s2
    scaled_there = to_core(scaled)
    normed2_pieces = along_line(quarter(scaled, 0))
    cot_far = gathered([after(piece, scaled) for piece in cot_pieces])
    normed2_near = (jnp.concatenate([scaled, scaled_there], axis=0) * norm_second).astype(
        bf16
    )
    cot_near = jnp.concatenate([mine(cotangent), other(cotangent)], axis=0)
    hidden_near, d_gu_near = ffn(normed2_near, cot_near)
    d_normed2_chip, d_normed2_there = summed(
        d_gu_near[:half], d_gu_near[half:], lambda part: by_transpose(part, w_gu_flat)
    )

    saved_beside = conv_forward(after(beside, d_gu_near))

    d_normed2 = d_normed2_chip + d_normed2_there
    gn2 = jnp.sum(d_normed2 * resid * s2, axis=0)
    weighted2 = d_normed2 * norm_second
    d_resid = (
        mine(cotangent).astype(f32)
        + s2 * weighted2
        - resid * s2**3 * jnp.mean(weighted2 * resid, axis=-1, keepdims=True)
    )
    d_resid_seq = ordered(d_resid, to_core(d_resid)).astype(bf16)
    d_resid_beside = to_side(d_resid)

    d_proj, gtaps = conv_backward(d_resid_seq, saved)
    d_normed1, d_normed1_there = summed(
        mine(d_proj), other(d_proj), lambda part: by_transpose(part, w_in_flat)
    )

    d_resid_beside = after(d_resid_beside, d_proj)
    d_resid_next = ordered(d_resid_beside, to_core(d_resid_beside)).astype(bf16)
    d_proj_beside, _ = conv_backward(d_resid_next, saved_beside)

    kept, *parts = conv_parts(
        lax.rem(along + jnp.arange(line, dtype=jnp.int32), line) * 2 + side,
        (normed1, d_resid_seq, d_proj, gated),
        (saved_beside[1], d_resid_next, d_proj_beside, saved_beside[7]),
        line,
        block,
    )
    parts = [to_line(part, k + 1) for k, part in enumerate(parts)]
    total = sum(parts, kept)
    grad_in = total[:, : 3 * chans].reshape(block, 3, chans)
    grad_out = total[:, 3 * chans :].T

    normed2_far = gathered([after(piece, d_resid) for piece in normed2_pieces])
    here, there = [], []
    for piece in range(2):
        gu_here, gu_there, down_here, down_there = far_grads(
            jnp.stack([place, along * 2 + 1 - side]),
            block,
            piece,
            normed2_far,
            cot_far,
            norm_second.reshape(1, width),
            normed2_near,
            cot_near,
            hidden_near,
            d_gu_near,
            w_gu_flat,
            w_down,
        )
        here.append((gu_here, down_here))
        there.append((to_side(gu_there), to_side(down_there)))
    grad_gu = jnp.concatenate([a[0] + b[0] for a, b in zip(here, there)], axis=2)
    grad_gu = grad_gu.swapaxes(0, 1)
    grad_down = jnp.concatenate([a[1] + b[1] for a, b in zip(here, there)], axis=0)

    d_normed1 = d_normed1 + d_normed1_there
    xf_mine, s1_mine = mine(xf), mine(s1)
    weighted1 = d_normed1 * norm_first
    grad_mine = (
        d_resid
        + s1_mine * weighted1
        - xf_mine * s1_mine**3 * jnp.mean(weighted1 * xf_mine, axis=-1, keepdims=True)
    )
    grad_tokens = ordered(grad_mine, to_core(grad_mine))

    hidden_late = after(hidden_near, d_proj)
    out, out_there = summed(
        hidden_late[:half],
        hidden_late[half:],
        lambda part: jnp.dot(part, w_down, preferred_element_type=f32),
    )
    out_mine = resid + (out + out_there)
    block_out = ordered(out_mine, to_core(out_mine)).astype(bf16)

    gn1 = jnp.sum(d_normed1 * xf_mine * s1_mine, axis=0)
    gains = jnp.concatenate([gn1, gn2])
    gains = gains + to_core(gains)
    small = jnp.concatenate([gains, gtaps.reshape(-1)])
    stride = 2
    while stride < dp:
        there = lax.ppermute(small, "dp", [(i, i ^ stride) for i in range(dp)])
        small = small + there
        stride *= 2
    small = small + to_side(small)
    return (
        block_out,
        grad_tokens,
        small[:width],
        grad_in,
        small[2 * width : 2 * width + gtaps.size].reshape(gtaps.shape),
        grad_out,
        small[width : 2 * width],
        grad_gu,
        grad_down,
    )


def solution(mesh):
    dp, tensor = mesh.shape["dp"], mesh.shape["tensor"]

    def body(*args):
        if gathers(dp, tensor, *args[0].shape, args[7].shape[0] * tensor):
            return body_gather(dp, tensor, *args)
        return body_scatter(*args)

    return jax.shard_map(
        body,
        mesh=mesh,
        in_specs=(
            P("dp", None),
            P(),
            P(None, None, "tensor"),
            P(None, "tensor"),
            P("tensor", None),
            P(),
            P(None, None, "tensor"),
            P("tensor", None),
            P("dp", None),
        ),
        out_specs=(
            P("dp", None),
            P("dp", None),
            P(),
            P("dp", None, "tensor"),
            P(None, "tensor"),
            P("tensor", "dp"),
            P(),
            P("dp", None, "tensor"),
            P("tensor", "dp"),
        ),
        check_vma=False,
    )
```
